32 devices in a mesh: replica: 2 (over x), shard: 16 (over z, y, core).
Axes of the slice: x: 2, y: 2, z: 4, core: 2. Of those that a mesh axis runs over, the one named last changes fastest.
Arguments:
- activations: bfloat16 [4096, 512], P(('replica', 'shard')), may hold values from -6 to 6
- cotangents: bfloat16 [4096, 8192], P(('replica', 'shard')), may hold values from -0.0078125 to 0.0078125
- statistics: float32 [2, 8192, 512], P(None, 'shard'), may hold values from -8 to 32, as said below
- roots: bfloat16 [2, 8192, 512], P(None, 'shard'), may hold values from -0.25 to 0.25
- ages: int32 [32], replicated, may hold values from 1 to 16
- refresh: int32 [32], replicated, may hold values 0 or 1
Outputs:
- update: bfloat16 [8192, 512], P('shard')
- new_statistics: float32 [2, 8192, 512], P(None, 'shard')
- new_roots: bfloat16 [2, 8192, 512], P(None, 'shard')
The draws below stay inside these ranges and needn't reach their ends.
Inputs may be any that keep to these rules, and one draw needn't show every extreme that they name: `statistics`: for each block k, rows k * 512 to (k + 1) * 512 - 1 of either layer hold a symmetric positive definite 512 x 512 matrix.
All inputs are finite; a program needn't handle non-finite values.
Results may differ from the reference program's by a relative error of at most 0.0064.
Values may be sent and summed in bfloat16 or wider, within the bound.
A program may use at most 128 MiB of HBM per device.

```python
import math
import jax
import jax.numpy as jnp
from jax import lax

D = 8192
B = 512
ITERS = 3
TOKENS = 4096
FACTORS = 32


def draw_statistics(key, part):
    base_key = jax.random.fold_in(key, 11)
    scale_key = jax.random.fold_in(key, 12)
    entries = jax.random.normal(base_key, (2, D // B, B, B), jnp.float32)
    spread = jnp.exp(jax.random.uniform(scale_key, (2, D // B, B), jnp.float32, 0.0, math.log(3.0)))
    inner_form = jnp.einsum('kbij,kblj->kbil', entries, entries, precision=lax.Precision.HIGHEST) / B
    inner_form = inner_form + 0.5 * jnp.eye(B, dtype=jnp.float32)
    blocks_full = spread[..., :, None] * inner_form * spread[..., None, :]
    return blocks_full.reshape(2, D, B)


def with_ends(result, stream_key, least, high):
    extent = result.shape
    place = [jax.random.randint(jax.random.fold_in(stream_key, axis), (), 0, extent[axis]) for axis in range(len(extent))]
    result = result.at[tuple(place)].set(least)
    longest = extent.index(max(extent))
    place[longest] = (place[longest] + 1) % extent[longest]
    return result.at[tuple(place)].set(high)


def with_spikes(drawn, stream_key, source, target, shards_of, factor):
    def block_of(position):
        return (jnp.arange(drawn.shape[position]) // (drawn.shape[position] // shards_of)).reshape((-1,) + (1,) * (drawn.ndim - 1 - position))

    one_side = jax.random.permutation(stream_key, shards_of)[block_of(target)]
    other_side = (block_of(target) + shards_of // 2) % shards_of
    return jnp.where((block_of(source) == one_side) | (block_of(source) == other_side), factor * drawn, drawn)


def block_levels(own_key, shape, split, least, high):
    level = 1.0
    for dim, blocks in split:
        draws = jax.random.uniform(jax.random.fold_in(jax.random.fold_in(own_key, 6), dim), (blocks,), jnp.float32, least / len(split), high / len(split))
        level = level * jnp.repeat(jnp.exp(draws), shape[dim] // blocks).reshape((-1,) + (1,) * (len(shape) - 1 - dim))
    return level


def scatter_about(rng, extent, scale, bound, pieces=(), kind=jnp.bfloat16):
    gain = block_levels(rng, extent, pieces, -0.22, 0.18) if pieces else 1.0
    array = jax.random.normal(rng, extent, jnp.float32) * scale * gain
    return jnp.minimum(jnp.maximum(array, -bound), bound).astype(kind)


def noise_with(rng, shape, scale, reach, pieces, heavy, kind=jnp.bfloat16):
    drawn = scale * jax.random.normal(rng, shape, jnp.float32)
    if pieces:
        drawn = drawn * block_levels(rng, shape, pieces, -0.22, 0.18)
    return jnp.clip(with_spikes(drawn, jax.random.fold_in(rng, 3), *heavy), -reach, reach).astype(kind)


def setup_inputs(seed: int = 0) -> dict:
    splits = jax.random.split(jax.random.key(seed), 7)
    activations = scatter_about(splits[0], (TOKENS, B), 1.0, 6.0, ((0, 32),))
    cotangents = noise_with(splits[1], (TOKENS, D), (TOKENS * B) ** -0.5, 0.0078125, ((0, 32),), (0, 1, 32, 2.75))
    statistics = draw_statistics(jax.random.fold_in(splits[6], 71), 0)
    roots = scatter_about(splits[3], (2, D, B), B ** -0.5, 0.25, ((1, 16),))
    ages = with_ends(jax.random.randint(splits[4], (FACTORS,), 1, 17), jax.random.fold_in(splits[4], 1), 1, 16).astype(jnp.int32)
    refresh = with_ends((jax.random.randint(splits[5], (FACTORS,), 0, 2) < 1).astype(jnp.int32), jax.random.fold_in(splits[5], 1), 0, 1)
    return {"activations": activations, "cotangents": cotangents, "statistics": statistics, "roots": roots, "ages": ages, "refresh": refresh}


decay_base = 0.9
tiny_term = 1e-06

def newton(matrix):
    identity = jnp.eye(matrix.shape[-1], dtype=jnp.float32)
    frobenius = jnp.sqrt(jnp.sum(matrix * matrix) + tiny_term)
    scaling = 2.5 / frobenius
    iterate = scaling ** 0.25 * identity
    residual_map = scaling * matrix
    for sweep_index in range(ITERS):
        factor = (5.0 * identity - residual_map) * 0.25
        iterate = jnp.matmul(iterate, factor, precision=lax.Precision.HIGHEST)
        square = jnp.matmul(factor, factor, precision=lax.Precision.HIGHEST)
        fourth = jnp.matmul(square, square, precision=lax.Precision.HIGHEST)
        residual_map = jnp.matmul(fourth, residual_map, precision=lax.Precision.HIGHEST)
    return iterate

def reference(activations, cotangents, statistics, roots, ages, refresh):
    block_count = D // B
    gradient = lax.dot_general(cotangents, activations, (((0,), (0,)), ((), ())), preferred_element_type=jnp.float32)
    grad_blocks = gradient.astype(jnp.bfloat16).reshape(block_count, B, B)
    wide_blocks = grad_blocks.astype(jnp.float32)
    left_gram = jnp.einsum('nij,nkj->nik', wide_blocks, wide_blocks, precision=lax.Precision.HIGHEST)
    right_gram = jnp.einsum('nji,njk->nik', wide_blocks, wide_blocks, precision=lax.Precision.HIGHEST)
    gram_pairs = jnp.stack([left_gram, right_gram], axis=1).reshape(2 * block_count, B, B)
    previous = statistics.reshape(2, block_count, B, B).transpose(1, 0, 2, 3).reshape(2 * block_count, B, B)
    decay_factor = (decay_base ** ages.astype(jnp.float32))[:, None, None]
    fresh_mask = (refresh == 1)[:, None, None]
    updated = jnp.where(fresh_mask, decay_factor * previous + (1.0 - decay_factor) * gram_pairs, previous)
    fresh_roots = lax.map(newton, updated).astype(jnp.bfloat16)
    old_roots = roots.reshape(2, block_count, B, B).transpose(1, 0, 2, 3).reshape(2 * block_count, B, B)
    root_all = jnp.where(fresh_mask, fresh_roots, old_roots).reshape(block_count, 2, B, B)
    left_roots = root_all[:, 0].astype(jnp.float32)
    right_roots = root_all[:, 1].astype(jnp.float32)
    mixed_blocks = jnp.einsum('nij,njk->nik', wide_blocks, right_roots, precision=lax.Precision.HIGHEST).astype(jnp.bfloat16)
    product = jnp.einsum('nij,njk->nik', left_roots, mixed_blocks.astype(jnp.float32), precision=lax.Precision.HIGHEST)
    update = (product * math.sqrt(B)).reshape(D, B).astype(jnp.bfloat16)
    new_statistics = updated.reshape(block_count, 2, B, B).transpose(1, 0, 2, 3).reshape(2, D, B)
    new_roots = root_all.transpose(1, 0, 2, 3).reshape(2, D, B)
    return (update, new_statistics, new_roots)
```

```python
import functools
import math

import jax
import jax.numpy as jnp
from jax import lax
from jax.experimental import pallas as pl
from jax.experimental.pallas import tpu as pltpu
from jax.sharding import PartitionSpec as P

ITERS = 3


decay_base = 0.9
tiny_term = 1e-06


def from_partner(x, axis, apart):
    return lax.ppermute(x, axis, [(i, i ^ 1 << apart) for i in range(lax.axis_size(axis))])


def as_sent(x):
    return jax.tree.map(lambda a: a.astype(jnp.bfloat16) if a.dtype == jnp.float32 else a, x)


def newton(matrix):
    identity = jnp.eye(matrix.shape[-1], dtype=jnp.float32)
    frobenius = jnp.sqrt(jnp.sum(matrix * matrix) + tiny_term)
    scaling = 2.5 / frobenius
    iterate = scaling**0.25 * identity
    residual_map = scaling * matrix
    for sweep_index in range(ITERS):
        factor = (5.0 * identity - residual_map) * 0.25
        iterate = jnp.matmul(iterate, factor, precision=lax.Precision.HIGHEST)
        square = jnp.matmul(factor, factor, precision=lax.Precision.HIGHEST)
        fourth = jnp.matmul(square, square, precision=lax.Precision.HIGHEST)
        residual_map = jnp.matmul(fourth, residual_map, precision=lax.Precision.HIGHEST)
    return iterate


def gram_pair(blocks):
    left_gram = jnp.einsum("nij,nkj->nik", blocks, blocks, preferred_element_type=jnp.float32)
    right_gram = jnp.einsum("nji,njk->nik", blocks, blocks, preferred_element_type=jnp.float32)
    return jnp.stack([left_gram, right_gram], axis=1)


def stat_swap(values, bit_number):
    return from_partner(values, "shard", bit_number)


def block_swap(values, bit_number):
    return jax.tree.map(
        lambda part, own: part.astype(own.dtype),
        from_partner(as_sent(values), "shard", bit_number),
        values,
    )


def team_block(values, mover, team_size):
    shard_index = lax.axis_index("shard")
    gathered = values
    for bit_number in range(team_size.bit_length() - 1):
        partner = mover(gathered, bit_number)
        upper_side = jnp.right_shift(shard_index, bit_number) % 2 == 1
        below = jnp.concatenate([partner, gathered], axis=1)
        above = jnp.concatenate([gathered, partner], axis=1)
        gathered = jnp.where(upper_side, below, above)
    return gathered


def general(activations, cotangents, statistics, roots, ages, refresh):
    tokens_here = activations.shape[0]
    block_order = activations.shape[1]
    full_width = cotangents.shape[1]
    shards = lax.axis_size("shard")
    copies = lax.axis_size("replica")
    rows_here = statistics.shape[1]
    piece_rows = rows_here // copies
    reordered = (
        cotangents.reshape(tokens_here, shards, copies, piece_rows)
        .transpose(0, 2, 1, 3)
        .reshape(tokens_here, full_width)
    )
    total_piece = lax.psum_scatter(
        lax.dot_general(
            reordered, activations, (((0,), (0,)), ((), ())), preferred_element_type=jnp.float32
        ),
        ("replica", "shard"),
        scatter_dimension=0,
        tiled=True,
    )
    gradient = lax.all_gather(total_piece.astype(jnp.bfloat16), "replica", axis=0, tiled=True)
    shard_index = lax.axis_index("shard")
    if rows_here < block_order:
        team_size = block_order // rows_here
        team_place = shard_index % team_size
        first_block = shard_index // team_size
        row_start = team_place * rows_here
        blocks_here = 1
        old_stats = team_block(statistics, stat_swap, team_size)[:, None]
        full_pair = team_block(jnp.stack([gradient, roots[1]]), block_swap, team_size)
        grad_blocks = full_pair[0][None]
        right_old = full_pair[1][None]

        def own_rows(blocks):
            return lax.dynamic_slice_in_dim(blocks[0], row_start, rows_here, 0)

    else:
        blocks_here = rows_here // block_order
        first_block = shard_index * blocks_here
        old_stats = statistics.reshape(2, blocks_here, block_order, block_order)
        grad_blocks = gradient.reshape(blocks_here, block_order, block_order)
        right_old = roots[1].reshape(blocks_here, block_order, block_order)

        def own_rows(blocks):
            return blocks.reshape(rows_here, blocks.shape[-1])

    count_here = 2 * blocks_here
    gram_pairs = gram_pair(grad_blocks).reshape(count_here, block_order, block_order)
    previous = old_stats.transpose(1, 0, 2, 3).reshape(count_here, block_order, block_order)
    ages_here = lax.dynamic_slice_in_dim(ages, 2 * first_block, count_here, 0)
    fresh_here = lax.dynamic_slice_in_dim(refresh, 2 * first_block, count_here, 0) == 1
    decay_factor = (decay_base ** ages_here.astype(jnp.float32))[:, None, None]
    updated = jnp.where(
        fresh_here[:, None, None],
        decay_factor * previous + (1.0 - decay_factor) * gram_pairs,
        previous,
    )
    refreshed = jax.vmap(newton)(updated).astype(jnp.bfloat16)
    root_pairs = refreshed.reshape(blocks_here, 2, block_order, block_order)
    fresh_pairs = fresh_here.reshape(blocks_here, 2)
    right_full = jnp.where(fresh_pairs[:, 1, None, None], root_pairs[:, 1], right_old)
    left_mask = own_rows(
        jnp.broadcast_to(fresh_pairs[:, 0, None, None], (blocks_here, block_order, 1))
    )
    left_rows = jnp.where(left_mask, own_rows(root_pairs[:, 0]), roots[0])
    new_roots = jnp.stack([left_rows, own_rows(right_full)])
    stat_pairs = updated.reshape(blocks_here, 2, block_order, block_order)
    new_statistics = jnp.stack([own_rows(stat_pairs[:, 0]), own_rows(stat_pairs[:, 1])])
    mixed_blocks = jnp.einsum(
        "nij,njk->nik", grad_blocks, right_full, preferred_element_type=jnp.float32
    ).astype(jnp.bfloat16)
    left_blocks = left_rows.reshape(blocks_here, -1, block_order)
    product = jnp.einsum(
        "nij,njk->nik", left_blocks, mixed_blocks, preferred_element_type=jnp.float32
    )
    update = (product.reshape(rows_here, block_order) * math.sqrt(block_order)).astype(jnp.bfloat16)
    return (update, new_statistics, new_roots)


CORES = 2
LANES = 2
MESH = pl.DeviceIdType.MESH


def exchange_kernel(
    sizes, cot_ref, act_ref, grad_ref, cots, acts, outgoing, incoming, grad,
    local_sem, act_send, act_recv, relay_send, cot_send, cot_recv,
    part_send, part_recv, grad_send, grad_recv,
):
    copies, levels, block, tokens, rows = sizes
    piece = rows // copies
    team = CORES * LANES
    here = lax.axis_index("replica")
    shard = lax.axis_index("shard")
    level = shard // team
    lane = (shard // CORES) % LANES
    core = shard % CORES
    slots = [(a, b, c) for a in range(copies) for b in range(LANES) for c in range(CORES)]

    def peer(offset):
        a, b, c = offset
        other = (level * LANES + (lane + b) % LANES) * CORES + (core + c) % CORES
        return ((here + a) % copies, other)

    def level_peer(step):
        return (here, ((level + step) % levels) * team + lane * CORES + core)

    def columns(device, step):
        target = ((level + step) % levels) * team + device[1] % team
        return pl.ds(pl.multiple_of(target * rows + device[0] * piece, piece), piece)

    barrier = pltpu.get_barrier_semaphore()
    for offset in slots[1:]:
        pl.semaphore_signal(barrier, inc=1, device_id=peer(offset), device_id_type=MESH)
    for step in range(1, levels):
        pl.semaphore_signal(barrier, inc=1, device_id=level_peer(step), device_id_type=MESH)
    own_act = pltpu.make_async_copy(act_ref, acts.at[pl.ds(0, tokens)], local_sem.at[0])
    own_act.start()
    own_cots = []
    for k in range(levels):
        own = pltpu.make_async_copy(
            cot_ref.at[:, columns((here, shard), k + 1)],
            cots.at[k, pl.ds(0, tokens)],
            local_sem.at[1 + k],
        )
        own.start()
        own_cots.append(own)
    pl.semaphore_wait(barrier, len(slots) - 1 + levels - 1)

    sends = []
    act_in = {}
    for index, offset in enumerate(slots):
        if index == 0:
            continue
        direct = offset[2] == 0 or offset == (0, 0, 1)
        copy = pltpu.make_async_remote_copy(
            src_ref=act_ref,
            dst_ref=acts.at[pl.ds(index * tokens, tokens)],
            send_sem=act_send.at[index],
            recv_sem=act_recv.at[index],
            device_id=peer(offset),
            device_id_type=MESH,
        )
        act_in[index] = copy
        if direct:
            copy.start()
            sends.append(copy)
    cot_in = {}
    for k in range(levels):
        for index, offset in enumerate(slots):
            if index == 0:
                continue
            device = peer(offset)
            copy = pltpu.make_async_remote_copy(
                src_ref=cot_ref.at[:, columns(device, k + 1)],
                dst_ref=cots.at[k, pl.ds(index * tokens, tokens)],
                send_sem=cot_send.at[k, index],
                recv_sem=cot_recv.at[k, index],
                device_id=device,
                device_id_type=MESH,
            )
            copy.start()
            sends.append(copy)
            cot_in[k, index] = copy
    for index, offset in enumerate(slots):
        if index == 0 or offset[2] != 0:
            continue
        act_in[index].wait_recv()
        relay = pltpu.make_async_remote_copy(
            src_ref=acts.at[pl.ds(index * tokens, tokens)],
            dst_ref=acts.at[pl.ds((index + 1) * tokens, tokens)],
            send_sem=relay_send.at[index],
            recv_sem=act_recv.at[index + 1],
            device_id=peer((0, 0, 1)),
            device_id_type=MESH,
        )
        relay.start()
        sends.append(relay)
    own_act.wait()
    for index, offset in enumerate(slots):
        if offset[2] != 0:
            act_in[index].wait_recv()

    parts = []
    for k in range(levels):
        own_cots[k].wait()
        for index in range(1, len(slots)):
            cot_in[k, index].wait_recv()
        part = lax.dot_general(
            cots[k], acts[...], (((0,), (0,)), ((), ())), preferred_element_type=jnp.float32
        )
        if k < levels - 1:
            outgoing[k] = part.astype(jnp.bfloat16)
            copy = pltpu.make_async_remote_copy(
                src_ref=outgoing.at[k],
                dst_ref=incoming.at[k],
                send_sem=part_send.at[k],
                recv_sem=part_recv.at[k],
                device_id=level_peer(k + 1),
                device_id_type=MESH,
            )
            copy.start()
            parts.append(copy)
    total = part
    for k in range(levels - 1):
        parts[k].wait_recv()
        total += incoming[k].astype(jnp.float32)
    mine = pl.ds(pl.multiple_of(here * piece, piece), piece)
    grad[mine] = total.astype(jnp.bfloat16)
    finals = []
    for step in range(1, copies):
        copy = pltpu.make_async_remote_copy(
            src_ref=grad.at[mine],
            dst_ref=grad.at[mine],
            send_sem=grad_send.at[step],
            recv_sem=grad_recv.at[step],
            device_id=((here + step) % copies, shard),
            device_id_type=MESH,
        )
        copy.start()
        finals.append(copy)
    for copy in sends + parts:
        copy.wait_send()
    for copy in finals:
        copy.wait()
    grad_ref[...] = grad[...]


def exchange(cotangents, activations, copies, levels, rows):
    tokens, block = activations.shape
    team = CORES * LANES
    many = copies * team
    piece = rows // copies
    dma = pltpu.SemaphoreType.DMA
    return pl.pallas_call(
        functools.partial(exchange_kernel, (copies, levels, block, tokens, rows)),
        out_shape=jax.ShapeDtypeStruct((rows, block), jnp.bfloat16),
        in_specs=[pl.BlockSpec(memory_space=pl.ANY), pl.BlockSpec(memory_space=pl.ANY)],
        out_specs=pl.BlockSpec(memory_space=pltpu.VMEM),
        scratch_shapes=[
            pltpu.VMEM((levels, many * tokens, piece), jnp.bfloat16),
            pltpu.VMEM((many * tokens, block), jnp.bfloat16),
            pltpu.VMEM((levels, piece, block), jnp.bfloat16),
            pltpu.VMEM((levels, piece, block), jnp.bfloat16),
            pltpu.VMEM((rows, block), jnp.bfloat16),
            dma((1 + levels,)),
            dma((many,)),
            dma((many,)),
            dma((many,)),
            dma((levels, many)),
            dma((levels, many)),
            dma((levels,)),
            dma((levels,)),
            dma((copies,)),
            dma((copies,)),
        ],
        compiler_params=pltpu.CompilerParams(collective_id=0, has_side_effects=True),
        name="exchange",
    )(cotangents, activations)


def product(left, right, contract=((1,), (0,))):
    return lax.dot_general(left, right, (contract, ((), ())), preferred_element_type=jnp.float32)


def small(x):
    return x.astype(jnp.bfloat16)


def root_step(n):
    half = small(n)
    q = product(half, half) - 2.5 * n
    half_q = small(q)
    r = product(half_q, half_q) + 3.125 * q
    return product(small(r), half) + 1.25**4 * n


def refresh_kernel(grad_ref, stats_ref, roots_ref, ages_ref, fresh_ref,
                   update_ref, new_stats_ref, new_roots_ref):
    first = 2 * lax.axis_index("shard")
    block = grad_ref.shape[0]
    grad = grad_ref[...]
    grams = [lambda: product(grad, grad, ((1,), (1,))), lambda: product(grad, grad, ((0,), (0,)))]
    maps, scales, fresh = [], [], []
    for side in range(2):
        is_fresh = fresh_ref[first + side] == 1
        age = jnp.full((1, 1), ages_ref[first + side].astype(jnp.float32), jnp.float32)
        decay = jnp.exp(age * math.log(decay_base))
        old = stats_ref[side]
        new = jnp.where(is_fresh, decay * old + (1.0 - decay) * grams[side](), old)
        new_stats_ref[side] = new
        total = jnp.sum(jnp.sum(new * new, axis=0, keepdims=True), axis=1, keepdims=True)
        scaling = 2.5 / jnp.sqrt(total + tiny_term)
        maps.append((0.25 * scaling) * new)
        scales.append(jnp.sqrt(jnp.sqrt(scaling)))
        fresh.append(is_fresh)
    n1 = maps
    n2 = [root_step(n) for n in n1]
    x2 = [product(small(a), small(b)) - 1.25 * (a + b) for a, b in zip(n1, n2)]
    n3 = [root_step(n) for n in n2]
    row = lax.broadcasted_iota(jnp.int32, (block, block), 0)
    column = lax.broadcasted_iota(jnp.int32, (block, block), 1)
    diagonal = jnp.where(row == column, 1.25**3, 0.0)
    roots = []
    for side in range(2):
        last = diagonal + 1.25 * x2[side] - 1.5625 * n3[side]
        last = last - product(small(x2[side]), small(n3[side]))
        root = small(scales[side] * last)
        root = jnp.where(fresh[side], root, roots_ref[side])
        new_roots_ref[side] = root
        roots.append(root)
    mixed = small(product(grad, roots[1]))
    update_ref[...] = small(product(roots[0], mixed) * math.sqrt(block))


def refresh_roots(gradient, statistics, roots, ages, refresh):
    vmem = pl.BlockSpec(memory_space=pltpu.VMEM)
    smem = pl.BlockSpec(memory_space=pltpu.SMEM)
    return pl.pallas_call(
        refresh_kernel,
        out_shape=(
            jax.ShapeDtypeStruct(gradient.shape, jnp.bfloat16),
            jax.ShapeDtypeStruct(statistics.shape, jnp.float32),
            jax.ShapeDtypeStruct(roots.shape, jnp.bfloat16),
        ),
        in_specs=[vmem, vmem, vmem, smem, smem],
        out_specs=(vmem, vmem, vmem),
        name="refresh_roots",
    )(gradient, statistics, roots, ages, refresh)


def per_device(activations, cotangents, statistics, roots, ages, refresh):
    shards = lax.axis_size("shard")
    copies = lax.axis_size("replica")
    rows = statistics.shape[1]
    block = activations.shape[1]
    team = CORES * LANES
    if rows != block or shards % team or rows % copies or (rows // copies) % 128:
        return general(activations, cotangents, statistics, roots, ages, refresh)
    gradient = exchange(cotangents, activations, copies, shards // team, rows)
    return refresh_roots(gradient, statistics, roots, ages, refresh)


def solution(mesh):
    in_specs = (
        P(("replica", "shard"), None),
        P(("replica", "shard"), None),
        P(None, "shard", None),
        P(None, "shard", None),
        P(),
        P(),
    )
    out_specs = (P("shard", None), P(None, "shard", None), P(None, "shard", None))
    return jax.shard_map(
        per_device, mesh=mesh, in_specs=in_specs, out_specs=out_specs, check_vma=False
    )
```

```python
import functools
import math

import jax
import jax.numpy as jnp
from jax import lax
from jax.experimental import pallas as pl
from jax.experimental.pallas import tpu as pltpu
from jax.sharding import PartitionSpec as P

ITERS = 3


decay_base = 0.9
tiny_term = 1e-06


def from_partner(x, axis, apart):
    return lax.ppermute(x, axis, [(i, i ^ 1 << apart) for i in range(lax.axis_size(axis))])


def as_sent(x):
    return jax.tree.map(lambda a: a.astype(jnp.bfloat16) if a.dtype == jnp.float32 else a, x)


def newton(matrix):
    identity = jnp.eye(matrix.shape[-1], dtype=jnp.float32)
    frobenius = jnp.sqrt(jnp.sum(matrix * matrix) + tiny_term)
    scaling = 2.5 / frobenius
    iterate = scaling**0.25 * identity
    residual_map = scaling * matrix
    for sweep_index in range(ITERS):
        factor = (5.0 * identity - residual_map) * 0.25
        iterate = jnp.matmul(iterate, factor, precision=lax.Precision.HIGHEST)
        square = jnp.matmul(factor, factor, precision=lax.Precision.HIGHEST)
        fourth = jnp.matmul(square, square, precision=lax.Precision.HIGHEST)
        residual_map = jnp.matmul(fourth, residual_map, precision=lax.Precision.HIGHEST)
    return iterate


def gram_pair(blocks):
    left_gram = jnp.einsum("nij,nkj->nik", blocks, blocks, preferred_element_type=jnp.float32)
    right_gram = jnp.einsum("nji,njk->nik", blocks, blocks, preferred_element_type=jnp.float32)
    return jnp.stack([left_gram, right_gram], axis=1)


def stat_swap(values, bit_number):
    return from_partner(values, "shard", bit_number)


def block_swap(values, bit_number):
    return jax.tree.map(
        lambda part, own: part.astype(own.dtype),
        from_partner(as_sent(values), "shard", bit_number),
        values,
    )


def team_block(values, mover, team_size):
    shard_index = lax.axis_index("shard")
    gathered = values
    for bit_number in range(team_size.bit_length() - 1):
        partner = mover(gathered, bit_number)
        upper_side = jnp.right_shift(shard_index, bit_number) % 2 == 1
        below = jnp.concatenate([partner, gathered], axis=1)
        above = jnp.concatenate([gathered, partner], axis=1)
        gathered = jnp.where(upper_side, below, above)
    return gathered


def general(activations, cotangents, statistics, roots, ages, refresh):
    tokens_here = activations.shape[0]
    block_order = activations.shape[1]
    full_width = cotangents.shape[1]
    shards = lax.axis_size("shard")
    copies = lax.axis_size("replica")
    rows_here = statistics.shape[1]
    piece_rows = rows_here // copies
    reordered = (
        cotangents.reshape(tokens_here, shards, copies, piece_rows)
        .transpose(0, 2, 1, 3)
        .reshape(tokens_here, full_width)
    )
    total_piece = lax.psum_scatter(
        lax.dot_general(
            reordered, activations, (((0,), (0,)), ((), ())), preferred_element_type=jnp.float32
        ),
        ("replica", "shard"),
        scatter_dimension=0,
        tiled=True,
    )
    gradient = lax.all_gather(total_piece.astype(jnp.bfloat16), "replica", axis=0, tiled=True)
    shard_index = lax.axis_index("shard")
    if rows_here < block_order:
        team_size = block_order // rows_here
        team_place = shard_index % team_size
        first_block = shard_index // team_size
        row_start = team_place * rows_here
        blocks_here = 1
        old_stats = team_block(statistics, stat_swap, team_size)[:, None]
        full_pair = team_block(jnp.stack([gradient, roots[1]]), block_swap, team_size)
        grad_blocks = full_pair[0][None]
        right_old = full_pair[1][None]

        def own_rows(blocks):
            return lax.dynamic_slice_in_dim(blocks[0], row_start, rows_here, 0)

    else:
        blocks_here = rows_here // block_order
        first_block = shard_index * blocks_here
        old_stats = statistics.reshape(2, blocks_here, block_order, block_order)
        grad_blocks = gradient.reshape(blocks_here, block_order, block_order)
        right_old = roots[1].reshape(blocks_here, block_order, block_order)

        def own_rows(blocks):
            return blocks.reshape(rows_here, blocks.shape[-1])

    count_here = 2 * blocks_here
    gram_pairs = gram_pair(grad_blocks).reshape(count_here, block_order, block_order)
    previous = old_stats.transpose(1, 0, 2, 3).reshape(count_here, block_order, block_order)
    ages_here = lax.dynamic_slice_in_dim(ages, 2 * first_block, count_here, 0)
    fresh_here = lax.dynamic_slice_in_dim(refresh, 2 * first_block, count_here, 0) == 1
    decay_factor = (decay_base ** ages_here.astype(jnp.float32))[:, None, None]
    updated = jnp.where(
        fresh_here[:, None, None],
        decay_factor * previous + (1.0 - decay_factor) * gram_pairs,
        previous,
    )
    refreshed = jax.vmap(newton)(updated).astype(jnp.bfloat16)
    root_pairs = refreshed.reshape(blocks_here, 2, block_order, block_order)
    fresh_pairs = fresh_here.reshape(blocks_here, 2)
    right_full = jnp.where(fresh_pairs[:, 1, None, None], root_pairs[:, 1], right_old)
    left_mask = own_rows(
        jnp.broadcast_to(fresh_pairs[:, 0, None, None], (blocks_here, block_order, 1))
    )
    left_rows = jnp.where(left_mask, own_rows(root_pairs[:, 0]), roots[0])
    new_roots = jnp.stack([left_rows, own_rows(right_full)])
    stat_pairs = updated.reshape(blocks_here, 2, block_order, block_order)
    new_statistics = jnp.stack([own_rows(stat_pairs[:, 0]), own_rows(stat_pairs[:, 1])])
    mixed_blocks = jnp.einsum(
        "nij,njk->nik", grad_blocks, right_full, preferred_element_type=jnp.float32
    ).astype(jnp.bfloat16)
    left_blocks = left_rows.reshape(blocks_here, -1, block_order)
    product = jnp.einsum(
        "nij,njk->nik", left_blocks, mixed_blocks, preferred_element_type=jnp.float32
    )
    update = (product.reshape(rows_here, block_order) * math.sqrt(block_order)).astype(jnp.bfloat16)
    return (update, new_statistics, new_roots)


CORES = 2
LANES = 2
SPLIT = 2
VMEM = 24 << 20
MESH = pl.DeviceIdType.MESH


def exchange_kernel(
    sizes, cot_ref, act_ref, grad_ref, cots, acts, outgoing, incoming, grad,
    local_sem, act_send, act_recv, relay_send, cot_send, cot_recv,
    part_send, part_recv, grad_send, grad_recv,
):
    copies, levels, tokens, rows = sizes
    piece = rows // copies
    part_rows = piece // SPLIT
    team = CORES * LANES
    here = lax.axis_index("replica")
    shard = lax.axis_index("shard")
    level = shard // team
    lane = (shard // CORES) % LANES
    core = shard % CORES
    slots = [(a, b, c) for a in range(copies) for b in range(LANES) for c in range(CORES)]
    steps = [(part, k) for part in range(SPLIT) for k in range(levels)]

    def peer(offset):
        a, b, c = offset
        other = (level * LANES + (lane + b) % LANES) * CORES + (core + c) % CORES
        return ((here + a) % copies, other)

    def level_peer(step):
        return (here, ((level + step) % levels) * team + lane * CORES + core)

    def columns(device, part, k):
        target = ((level + k + 1) % levels) * team + device[1] % team
        start = target * rows + device[0] * piece + part * part_rows
        return pl.ds(pl.multiple_of(start, part_rows), part_rows)

    def token_rows(index):
        return pl.ds(index * tokens, tokens)

    barrier = pltpu.get_barrier_semaphore()
    for offset in slots[1:]:
        pl.semaphore_signal(barrier, inc=1, device_id=peer(offset), device_id_type=MESH)
    for step in range(1, levels):
        pl.semaphore_signal(barrier, inc=1, device_id=level_peer(step), device_id_type=MESH)
    own_act = pltpu.make_async_copy(act_ref, acts.at[token_rows(0)], local_sem.at[0])
    own_act.start()
    own_cots = []
    for turn, (part, k) in enumerate(steps):
        own = pltpu.make_async_copy(
            cot_ref.at[:, columns((here, shard), part, k)],
            cots.at[turn, token_rows(0)],
            local_sem.at[1 + turn],
        )
        own.start()
        own_cots.append(own)
    pl.semaphore_wait(barrier, len(slots) - 1 + levels - 1)

    sends = []

    def send_act(offset, direct, via):
        index = slots.index(offset)
        first = slots.index(tuple(o - v for o, v in zip(offset, via)))
        copy = pltpu.make_async_remote_copy(
            src_ref=act_ref if direct else acts.at[token_rows(first)],
            dst_ref=acts.at[token_rows(index)],
            send_sem=act_send.at[index],
            recv_sem=act_recv.at[index],
            device_id=peer(via),
            device_id_type=MESH,
        )
        copy.start()
        sends.append(copy)
        return copy

    cot_in = {}

    def send_cots(turns):
        for turn in turns:
            for index in range(1, len(slots)):
                device = peer(slots[index])
                copy = pltpu.make_async_remote_copy(
                    src_ref=cot_ref.at[:, columns(device, *steps[turn])],
                    dst_ref=cots.at[turn, token_rows(index)],
                    send_sem=cot_send.at[turn, index],
                    recv_sem=cot_recv.at[turn, index],
                    device_id=device,
                    device_id_type=MESH,
                )
                copy.start()
                sends.append(copy)
                cot_in[turn, index] = copy

    act_in = {}
    for a in range(1, copies):
        act_in[a, 0, 0] = send_act((a, 0, 0), True, (a, 0, 0))
    for b in range(1, LANES):
        act_in[0, b, 0] = send_act((0, b, 0), True, (0, b, 0))
    for c in range(1, CORES):
        act_in[0, 0, c] = send_act((0, 0, c), True, (0, 0, c))
    send_cots(range(1))
    for a in range(1, copies):
        act_in[a, 0, 0].wait_recv()
        for b in range(1, LANES):
            act_in[a, b, 0] = send_act((a, b, 0), False, (0, b, 0))
    send_cots(range(1, len(steps)))
    for a in range(copies):
        for b in range(LANES):
            if b:
                act_in[a, b, 0].wait_recv()
            if a or b:
                for c in range(1, CORES):
                    act_in[a, b, c] = send_act((a, b, c), False, (0, 0, c))
    own_act.wait()
    for offset in slots:
        if offset[2]:
            act_in[offset].wait_recv()

    parts, finals = {}, []
    for turn, (part, k) in enumerate(steps):
        own_cots[turn].wait()
        for index in range(1, len(slots)):
            cot_in[turn, index].wait_recv()
        term = lax.dot_general(
            cots[turn], acts[...], (((0,), (0,)), ((), ())), preferred_element_type=jnp.float32
        )
        if k < levels - 1:
            outgoing[turn] = term.astype(jnp.bfloat16)
            copy = pltpu.make_async_remote_copy(
                src_ref=outgoing.at[turn],
                dst_ref=incoming.at[turn],
                send_sem=part_send.at[turn],
                recv_sem=part_recv.at[turn],
                device_id=level_peer(k + 1),
                device_id_type=MESH,
            )
            copy.start()
            sends.append(copy)
            parts[turn] = copy
            continue
        for other in range(part * levels, turn):
            parts[other].wait_recv()
            term += incoming[other].astype(jnp.float32)
        start = here * piece + part * part_rows
        mine = pl.ds(pl.multiple_of(start, part_rows), part_rows)
        grad[mine] = term.astype(jnp.bfloat16)
        for step in range(1, copies):
            copy = pltpu.make_async_remote_copy(
                src_ref=grad.at[mine],
                dst_ref=grad.at[mine],
                send_sem=grad_send.at[part, step],
                recv_sem=grad_recv.at[part, step],
                device_id=((here + step) % copies, shard),
                device_id_type=MESH,
            )
            copy.start()
            finals.append(copy)
    for copy in sends:
        copy.wait_send()
    for copy in finals:
        copy.wait()
    grad_ref[...] = grad[...]


def exchange(cotangents, activations, copies, levels, rows):
    tokens, block = activations.shape
    team = CORES * LANES
    many = copies * team
    turns = SPLIT * levels
    part_rows = rows // copies // SPLIT
    dma = pltpu.SemaphoreType.DMA
    return pl.pallas_call(
        functools.partial(exchange_kernel, (copies, levels, tokens, rows)),
        out_shape=jax.ShapeDtypeStruct((rows, block), jnp.bfloat16),
        in_specs=[pl.BlockSpec(memory_space=pltpu.HBM)] * 2,
        out_specs=pl.BlockSpec(memory_space=pltpu.VMEM),
        scratch_shapes=[
            pltpu.VMEM((turns, many * tokens, part_rows), jnp.bfloat16),
            pltpu.VMEM((many * tokens, block), jnp.bfloat16),
            pltpu.VMEM((turns, part_rows, block), jnp.bfloat16),
            pltpu.VMEM((turns, part_rows, block), jnp.bfloat16),
            pltpu.VMEM((rows, block), jnp.bfloat16),
            dma((1 + turns,)),
            dma((many,)),
            dma((many,)),
            dma((many,)),
            dma((turns, many)),
            dma((turns, many)),
            dma((turns,)),
            dma((turns,)),
            dma((SPLIT, copies)),
            dma((SPLIT, copies)),
        ],
        compiler_params=pltpu.CompilerParams(collective_id=0, has_side_effects=True, vmem_limit_bytes=VMEM),
        name="exchange",
    )(cotangents, activations)


def product(left, right, contract=((1,), (0,))):
    return lax.dot_general(left, right, (contract, ((), ())), preferred_element_type=jnp.float32)


def small(x):
    return x.astype(jnp.bfloat16)


def root_step(n):
    half = small(n)
    q = product(half, half) - 2.5 * n
    half_q = small(q)
    r = product(half_q, half_q) + 3.125 * q
    return product(small(r), half) + 1.25**4 * n


def refresh_kernel(grad_ref, stats_ref, roots_ref, ages_ref, fresh_ref,
                   update_out, new_stats_out, new_roots_out,
                   update_ref, new_stats_ref, new_roots_ref, old_roots_ref, sem):
    old_roots = pltpu.make_async_copy(roots_ref, old_roots_ref, sem.at[5])
    old_roots.start()
    pending = []

    def put(source, target):
        copy = pltpu.make_async_copy(source, target, sem.at[len(pending)])
        copy.start()
        pending.append(copy)

    first = 2 * lax.axis_index("shard")
    block = grad_ref.shape[0]
    grad = grad_ref[...]
    grams = [lambda: product(grad, grad, ((1,), (1,))), lambda: product(grad, grad, ((0,), (0,)))]
    maps, scales, fresh = [], [], []
    for side in range(2):
        is_fresh = fresh_ref[first + side] == 1
        age = jnp.full((1, 1), ages_ref[first + side].astype(jnp.float32), jnp.float32)
        decay = jnp.exp(age * math.log(decay_base))
        old = stats_ref[side]
        new = jnp.where(is_fresh, decay * old + (1.0 - decay) * grams[side](), old)
        new_stats_ref[side] = new
        put(new_stats_ref.at[side], new_stats_out.at[side])
        total = jnp.sum(jnp.sum(new * new, axis=0, keepdims=True), axis=1, keepdims=True)
        scaling = 2.5 / jnp.sqrt(total + tiny_term)
        maps.append((0.25 * scaling) * new)
        scales.append(jnp.sqrt(jnp.sqrt(scaling)))
        fresh.append(is_fresh)
    n1 = maps
    n2 = [root_step(n) for n in n1]
    x2 = [product(small(a), small(b)) - 1.25 * (a + b) for a, b in zip(n1, n2)]
    n3 = [root_step(n) for n in n2]
    row = lax.broadcasted_iota(jnp.int32, (block, block), 0)
    column = lax.broadcasted_iota(jnp.int32, (block, block), 1)
    diagonal = jnp.where(row == column, 1.25**3, 0.0)
    roots = []
    old_roots.wait()
    for side in range(2):
        last = diagonal + 1.25 * x2[side] - 1.5625 * n3[side]
        last = last - product(small(x2[side]), small(n3[side]))
        root = small(scales[side] * last)
        root = jnp.where(fresh[side], root, old_roots_ref[side])
        new_roots_ref[side] = root
        put(new_roots_ref.at[side], new_roots_out.at[side])
        roots.append(root)
    mixed = small(product(grad, roots[1]))
    update_ref[...] = small(product(roots[0], mixed) * math.sqrt(block))
    put(update_ref, update_out)
    for copy in pending:
        copy.wait()


def refresh_roots(gradient, statistics, roots, ages, refresh):
    vmem = pl.BlockSpec(memory_space=pltpu.VMEM)
    smem = pl.BlockSpec(memory_space=pltpu.SMEM)
    hbm = pl.BlockSpec(memory_space=pltpu.HBM)
    return pl.pallas_call(
        refresh_kernel,
        out_shape=(
            jax.ShapeDtypeStruct(gradient.shape, jnp.bfloat16),
            jax.ShapeDtypeStruct(statistics.shape, jnp.float32),
            jax.ShapeDtypeStruct(roots.shape, jnp.bfloat16),
        ),
        in_specs=[vmem, vmem, hbm, smem, smem],
        out_specs=(hbm,) * 3,
        scratch_shapes=[
            pltpu.VMEM(gradient.shape, jnp.bfloat16),
            pltpu.VMEM(statistics.shape, jnp.float32),
            pltpu.VMEM(roots.shape, jnp.bfloat16),
            pltpu.VMEM(roots.shape, jnp.bfloat16),
            pltpu.SemaphoreType.DMA((6,)),
        ],
        compiler_params=pltpu.CompilerParams(vmem_limit_bytes=VMEM),
        name="refresh_roots",
    )(gradient, statistics, roots, ages, refresh)


def per_device(activations, cotangents, statistics, roots, ages, refresh):
    shards = lax.axis_size("shard")
    copies = lax.axis_size("replica")
    rows = statistics.shape[1]
    block = activations.shape[1]
    team = CORES * LANES
    if rows != block or shards % team or rows % copies or (rows // copies) % (128 * SPLIT):
        return general(activations, cotangents, statistics, roots, ages, refresh)
    gradient = exchange(cotangents, activations, copies, shards // team, rows)
    return refresh_roots(gradient, statistics, roots, ages, refresh)


def solution(mesh):
    in_specs = (
        P(("replica", "shard"), None),
        P(("replica", "shard"), None),
        P(None, "shard", None),
        P(None, "shard", None),
        P(),
        P(),
    )
    out_specs = (P("shard", None), P(None, "shard", None), P(None, "shard", None))
    return jax.shard_map(
        per_device, mesh=mesh, in_specs=in_specs, out_specs=out_specs, check_vma=False
    )
```

```python
import functools
import math

import jax
import jax.numpy as jnp
from jax import lax
from jax.experimental import pallas as pl
from jax.experimental.pallas import tpu as pltpu
from jax.sharding import PartitionSpec as P

ITERS = 3


decay_base = 0.9
tiny_term = 1e-06


def from_partner(x, axis, apart):
    return lax.ppermute(x, axis, [(i, i ^ 1 << apart) for i in range(lax.axis_size(axis))])


def as_sent(x):
    return jax.tree.map(lambda a: a.astype(jnp.bfloat16) if a.dtype == jnp.float32 else a, x)


def newton(matrix):
    identity = jnp.eye(matrix.shape[-1], dtype=jnp.float32)
    frobenius = jnp.sqrt(jnp.sum(matrix * matrix) + tiny_term)
    scaling = 2.5 / frobenius
    iterate = scaling**0.25 * identity
    residual_map = scaling * matrix
    for sweep_index in range(ITERS):
        factor = (5.0 * identity - residual_map) * 0.25
        iterate = jnp.matmul(iterate, factor, precision=lax.Precision.HIGHEST)
        square = jnp.matmul(factor, factor, precision=lax.Precision.HIGHEST)
        fourth = jnp.matmul(square, square, precision=lax.Precision.HIGHEST)
        residual_map = jnp.matmul(fourth, residual_map, precision=lax.Precision.HIGHEST)
    return iterate


def gram_pair(blocks):
    left_gram = jnp.einsum("nij,nkj->nik", blocks, blocks, preferred_element_type=jnp.float32)
    right_gram = jnp.einsum("nji,njk->nik", blocks, blocks, preferred_element_type=jnp.float32)
    return jnp.stack([left_gram, right_gram], axis=1)


def stat_swap(values, bit_number):
    return from_partner(values, "shard", bit_number)


def block_swap(values, bit_number):
    return jax.tree.map(
        lambda part, own: part.astype(own.dtype),
        from_partner(as_sent(values), "shard", bit_number),
        values,
    )


def team_block(values, mover, team_size):
    shard_index = lax.axis_index("shard")
    gathered = values
    for bit_number in range(team_size.bit_length() - 1):
        partner = mover(gathered, bit_number)
        upper_side = jnp.right_shift(shard_index, bit_number) % 2 == 1
        below = jnp.concatenate([partner, gathered], axis=1)
        above = jnp.concatenate([gathered, partner], axis=1)
        gathered = jnp.where(upper_side, below, above)
    return gathered


def general(activations, cotangents, statistics, roots, ages, refresh):
    tokens_here = activations.shape[0]
    block_order = activations.shape[1]
    full_width = cotangents.shape[1]
    shards = lax.axis_size("shard")
    copies = lax.axis_size("replica")
    rows_here = statistics.shape[1]
    piece_rows = rows_here // copies
    reordered = (
        cotangents.reshape(tokens_here, shards, copies, piece_rows)
        .transpose(0, 2, 1, 3)
        .reshape(tokens_here, full_width)
    )
    total_piece = lax.psum_scatter(
        lax.dot_general(
            reordered, activations, (((0,), (0,)), ((), ())), preferred_element_type=jnp.float32
        ),
        ("replica", "shard"),
        scatter_dimension=0,
        tiled=True,
    )
    gradient = lax.all_gather(total_piece.astype(jnp.bfloat16), "replica", axis=0, tiled=True)
    shard_index = lax.axis_index("shard")
    if rows_here < block_order:
        team_size = block_order // rows_here
        team_place = shard_index % team_size
        first_block = shard_index // team_size
        row_start = team_place * rows_here
        blocks_here = 1
        old_stats = team_block(statistics, stat_swap, team_size)[:, None]
        full_pair = team_block(jnp.stack([gradient, roots[1]]), block_swap, team_size)
        grad_blocks = full_pair[0][None]
        right_old = full_pair[1][None]

        def own_rows(blocks):
            return lax.dynamic_slice_in_dim(blocks[0], row_start, rows_here, 0)

    else:
        blocks_here = rows_here // block_order
        first_block = shard_index * blocks_here
        old_stats = statistics.reshape(2, blocks_here, block_order, block_order)
        grad_blocks = gradient.reshape(blocks_here, block_order, block_order)
        right_old = roots[1].reshape(blocks_here, block_order, block_order)

        def own_rows(blocks):
            return blocks.reshape(rows_here, blocks.shape[-1])

    count_here = 2 * blocks_here
    gram_pairs = gram_pair(grad_blocks).reshape(count_here, block_order, block_order)
    previous = old_stats.transpose(1, 0, 2, 3).reshape(count_here, block_order, block_order)
    ages_here = lax.dynamic_slice_in_dim(ages, 2 * first_block, count_here, 0)
    fresh_here = lax.dynamic_slice_in_dim(refresh, 2 * first_block, count_here, 0) == 1
    decay_factor = (decay_base ** ages_here.astype(jnp.float32))[:, None, None]
    updated = jnp.where(
        fresh_here[:, None, None],
        decay_factor * previous + (1.0 - decay_factor) * gram_pairs,
        previous,
    )
    refreshed = jax.vmap(newton)(updated).astype(jnp.bfloat16)
    root_pairs = refreshed.reshape(blocks_here, 2, block_order, block_order)
    fresh_pairs = fresh_here.reshape(blocks_here, 2)
    right_full = jnp.where(fresh_pairs[:, 1, None, None], root_pairs[:, 1], right_old)
    left_mask = own_rows(
        jnp.broadcast_to(fresh_pairs[:, 0, None, None], (blocks_here, block_order, 1))
    )
    left_rows = jnp.where(left_mask, own_rows(root_pairs[:, 0]), roots[0])
    new_roots = jnp.stack([left_rows, own_rows(right_full)])
    stat_pairs = updated.reshape(blocks_here, 2, block_order, block_order)
    new_statistics = jnp.stack([own_rows(stat_pairs[:, 0]), own_rows(stat_pairs[:, 1])])
    mixed_blocks = jnp.einsum(
        "nij,njk->nik", grad_blocks, right_full, preferred_element_type=jnp.float32
    ).astype(jnp.bfloat16)
    left_blocks = left_rows.reshape(blocks_here, -1, block_order)
    product = jnp.einsum(
        "nij,njk->nik", left_blocks, mixed_blocks, preferred_element_type=jnp.float32
    )
    update = (product.reshape(rows_here, block_order) * math.sqrt(block_order)).astype(jnp.bfloat16)
    return (update, new_statistics, new_roots)


CORES = 2
LANES = 2
LEVELS = 4
SPLIT = 2
MESH = pl.DeviceIdType.MESH


def exchange_kernel(
    sizes, cot_ref, act_ref, grad_ref, cots, acts, outgoing, incoming, grad,
    local_sem, act_send, act_recv, relay_send, cot_send, cot_recv,
    part_send, part_recv, grad_send, grad_recv,
):
    copies, levels, tokens, rows = sizes
    piece = rows // copies
    part_rows = piece // SPLIT
    team = CORES * LANES
    here = lax.axis_index("replica")
    shard = lax.axis_index("shard")
    level = shard // team
    lane = (shard // CORES) % LANES
    core = shard % CORES
    slots = [(a, b, c) for a in range(copies) for b in range(LANES) for c in range(CORES)]
    steps = [(part, k) for k in range(levels) for part in range(SPLIT)]

    def peer(offset):
        a, b, c = offset
        other = (level * LANES + (lane + b) % LANES) * CORES + (core + c) % CORES
        return ((here + a) % copies, other)

    beside = level + 1 - 2 * (level % 2)
    targets = [(beside + 2) % levels, (level + 2) % levels, beside, level]
    receivers = [beside, (level + 2) % levels, beside]

    def level_peer(other):
        return (here, other * team + lane * CORES + core)

    def columns(device, part, k):
        target = targets[k] * team + device[1] % team
        start = target * rows + device[0] * piece + part * part_rows
        return pl.ds(pl.multiple_of(start, part_rows), part_rows)

    def token_rows(index):
        return pl.ds(index * tokens, tokens)

    barrier = pltpu.get_barrier_semaphore()
    for offset in slots[1:]:
        pl.semaphore_signal(barrier, inc=1, device_id=peer(offset), device_id_type=MESH)
    for other in receivers[:2]:
        pl.semaphore_signal(barrier, inc=1, device_id=level_peer(other), device_id_type=MESH)
    own_act = pltpu.make_async_copy(act_ref, acts.at[token_rows(0)], local_sem.at[0])
    own_act.start()
    own_cots = []
    for turn, (part, k) in enumerate(steps):
        own = pltpu.make_async_copy(
            cot_ref.at[:, columns((here, shard), part, k)],
            cots.at[turn, token_rows(0)],
            local_sem.at[1 + turn],
        )
        own.start()
        own_cots.append(own)
    pl.semaphore_wait(barrier, len(slots) - 1 + 2)

    sends = []

    def send_act(offset, direct, via):
        index = slots.index(offset)
        first = slots.index(tuple(o - v for o, v in zip(offset, via)))
        copy = pltpu.make_async_remote_copy(
            src_ref=act_ref if direct else acts.at[token_rows(first)],
            dst_ref=acts.at[token_rows(index)],
            send_sem=act_send.at[index],
            recv_sem=act_recv.at[index],
            device_id=peer(via),
            device_id_type=MESH,
        )
        copy.start()
        sends.append(copy)
        return copy

    cot_in = {}

    def send_cots(turns):
        for turn in turns:
            for index in range(1, len(slots)):
                device = peer(slots[index])
                copy = pltpu.make_async_remote_copy(
                    src_ref=cot_ref.at[:, columns(device, *steps[turn])],
                    dst_ref=cots.at[turn, token_rows(index)],
                    send_sem=cot_send.at[turn, index],
                    recv_sem=cot_recv.at[turn, index],
                    device_id=device,
                    device_id_type=MESH,
                )
                copy.start()
                sends.append(copy)
                cot_in[turn, index] = copy

    act_in = {}
    for offset in slots[1:]:
        if not offset[2] or offset[:2] == (0, 0):
            act_in[offset] = send_act(offset, True, offset)
    send_cots(range(len(steps)))
    for a, b, c in slots[1:]:
        if c and (a or b):
            if c == 1:
                act_in[a, b, 0].wait_recv()
            act_in[a, b, c] = send_act((a, b, c), False, (0, 0, c))
    own_act.wait()
    for offset in slots:
        if offset[2]:
            act_in[offset].wait_recv()

    parts, finals = {}, []
    for turn, (part, k) in enumerate(steps):
        own_cots[turn].wait()
        for index in range(1, len(slots)):
            cot_in[turn, index].wait_recv()
        term = lax.dot_general(
            cots[turn], acts[...], (((0,), (0,)), ((), ())), preferred_element_type=jnp.float32
        )
        if k == 1:
            parts[part, 0].wait_recv()
            term += incoming[part].astype(jnp.float32)
        if k < levels - 1:
            outgoing[turn] = term.astype(jnp.bfloat16)
            copy = pltpu.make_async_remote_copy(
                src_ref=outgoing.at[turn],
                dst_ref=incoming.at[turn],
                send_sem=part_send.at[turn],
                recv_sem=part_recv.at[turn],
                device_id=level_peer(receivers[k]),
                device_id_type=MESH,
            )
            copy.start()
            sends.append(copy)
            parts[part, k] = copy
            continue
        for other in range(1, k):
            parts[part, other].wait_recv()
            term += incoming[other * SPLIT + part].astype(jnp.float32)
        start = here * piece + part * part_rows
        mine = pl.ds(pl.multiple_of(start, part_rows), part_rows)
        grad[mine] = term.astype(jnp.bfloat16)
        for step in range(1, copies):
            copy = pltpu.make_async_remote_copy(
                src_ref=grad.at[mine],
                dst_ref=grad.at[mine],
                send_sem=grad_send.at[part, step],
                recv_sem=grad_recv.at[part, step],
                device_id=((here + step) % copies, shard),
                device_id_type=MESH,
            )
            copy.start()
            finals.append(copy)
    for copy in sends:
        copy.wait_send()
    for copy in finals:
        copy.wait()
    grad_ref[...] = grad[...]


def exchange(cotangents, activations, copies, levels, rows):
    tokens, block = activations.shape
    team = CORES * LANES
    many = copies * team
    turns = SPLIT * levels
    part_rows = rows // copies // SPLIT
    dma = pltpu.SemaphoreType.DMA
    return pl.pallas_call(
        functools.partial(exchange_kernel, (copies, levels, tokens, rows)),
        out_shape=jax.ShapeDtypeStruct((rows, block), jnp.bfloat16),
        in_specs=[pl.BlockSpec(memory_space=pltpu.HBM)] * 2,
        out_specs=pl.BlockSpec(memory_space=pltpu.VMEM),
        scratch_shapes=[
            pltpu.VMEM((turns, many * tokens, part_rows), jnp.bfloat16),
            pltpu.VMEM((many * tokens, block), jnp.bfloat16),
            pltpu.VMEM((turns, part_rows, block), jnp.bfloat16),
            pltpu.VMEM((turns, part_rows, block), jnp.bfloat16),
            pltpu.VMEM((rows, block), jnp.bfloat16),
            dma((1 + turns,)),
            dma((many,)),
            dma((many,)),
            dma((many,)),
            dma((turns, many)),
            dma((turns, many)),
            dma((turns,)),
            dma((turns,)),
            dma((SPLIT, copies)),
            dma((SPLIT, copies)),
        ],
        compiler_params=pltpu.CompilerParams(collective_id=0, has_side_effects=True),
        name="exchange",
    )(cotangents, activations)


def product(left, right, contract=((1,), (0,))):
    return lax.dot_general(left, right, (contract, ((), ())), preferred_element_type=jnp.float32)


def small(x):
    return x.astype(jnp.bfloat16)


def root_step(n):
    half = small(n)
    q = product(half, half) - 2.5 * n
    half_q = small(q)
    r = product(half_q, half_q) + 3.125 * q
    return product(small(r), half) + 1.25**4 * n


def refresh_kernel(grad_ref, stats_ref, roots_ref, ages_ref, fresh_ref,
                   update_out, new_stats_out, new_roots_out,
                   update_ref, new_stats_ref, new_roots_ref, old_stats_ref, old_roots_ref, sem):
    old_roots = pltpu.make_async_copy(roots_ref, old_roots_ref, sem.at[5])
    old_stats = []
    for side in range(2):
        load = pltpu.make_async_copy(stats_ref.at[side], old_stats_ref.at[side], sem.at[6 + side])
        load.start()
        old_stats.append(load)
    old_roots.start()
    pending = []

    def put(source, target):
        copy = pltpu.make_async_copy(source, target, sem.at[len(pending)])
        copy.start()
        pending.append(copy)

    first = 2 * lax.axis_index("shard")
    block = grad_ref.shape[0]
    grad = grad_ref[...]
    grams = [lambda: product(grad, grad, ((1,), (1,))), lambda: product(grad, grad, ((0,), (0,)))]
    maps, scales, fresh = [], [], []
    for side in range(2):
        is_fresh = fresh_ref[first + side] == 1
        age = jnp.full((1, 1), ages_ref[first + side].astype(jnp.float32), jnp.float32)
        decay = jnp.exp(age * math.log(decay_base))
        gram = grams[side]()
        old_stats[side].wait()
        old = old_stats_ref[side]
        new = jnp.where(is_fresh, decay * old + (1.0 - decay) * gram, old)
        new_stats_ref[side] = new
        put(new_stats_ref.at[side], new_stats_out.at[side])
        total = jnp.sum(jnp.sum(new * new, axis=0, keepdims=True), axis=1, keepdims=True)
        scaling = 2.5 / jnp.sqrt(total + tiny_term)
        maps.append((0.25 * scaling) * new)
        scales.append(jnp.sqrt(jnp.sqrt(scaling)))
        fresh.append(is_fresh)
    n1 = maps
    n2 = [root_step(n) for n in n1]
    x2 = [product(small(a), small(b)) - 1.25 * (a + b) for a, b in zip(n1, n2)]
    n3 = [root_step(n) for n in n2]
    row = lax.broadcasted_iota(jnp.int32, (block, block), 0)
    column = lax.broadcasted_iota(jnp.int32, (block, block), 1)
    diagonal = jnp.where(row == column, 1.25**3, 0.0)
    roots = []
    old_roots.wait()
    for side in range(2):
        last = diagonal + 1.25 * x2[side] - 1.5625 * n3[side]
        last = last - product(small(x2[side]), small(n3[side]))
        root = small(scales[side] * last)
        root = jnp.where(fresh[side], root, old_roots_ref[side])
        new_roots_ref[side] = root
        put(new_roots_ref.at[side], new_roots_out.at[side])
        roots.append(root)
    mixed = small(product(grad, roots[1]))
    update_ref[...] = small(product(roots[0], mixed) * math.sqrt(block))
    put(update_ref, update_out)
    for copy in pending:
        copy.wait()


def refresh_roots(gradient, statistics, roots, ages, refresh):
    vmem = pl.BlockSpec(memory_space=pltpu.VMEM)
    smem = pl.BlockSpec(memory_space=pltpu.SMEM)
    hbm = pl.BlockSpec(memory_space=pltpu.HBM)
    return pl.pallas_call(
        refresh_kernel,
        out_shape=(
            jax.ShapeDtypeStruct(gradient.shape, jnp.bfloat16),
            jax.ShapeDtypeStruct(statistics.shape, jnp.float32),
            jax.ShapeDtypeStruct(roots.shape, jnp.bfloat16),
        ),
        in_specs=[vmem, hbm, hbm, smem, smem],
        out_specs=(hbm,) * 3,
        scratch_shapes=[
            pltpu.VMEM(gradient.shape, jnp.bfloat16),
            pltpu.VMEM(statistics.shape, jnp.float32),
            pltpu.VMEM(roots.shape, jnp.bfloat16),
            pltpu.VMEM(statistics.shape, jnp.float32),
            pltpu.VMEM(roots.shape, jnp.bfloat16),
            pltpu.SemaphoreType.DMA((8,)),
        ],
        name="refresh_roots",
    )(gradient, statistics, roots, ages, refresh)


def per_device(activations, cotangents, statistics, roots, ages, refresh):
    shards = lax.axis_size("shard")
    copies = lax.axis_size("replica")
    rows = statistics.shape[1]
    block = activations.shape[1]
    team = CORES * LANES
    if rows != block or shards != LEVELS * team or rows % copies or (rows // copies) % (128 * SPLIT):
        return general(activations, cotangents, statistics, roots, ages, refresh)
    gradient = exchange(cotangents, activations, copies, shards // team, rows)
    return refresh_roots(gradient, statistics, roots, ages, refresh)


def solution(mesh):
    in_specs = (
        P(("replica", "shard"), None),
        P(("replica", "shard"), None),
        P(None, "shard", None),
        P(None, "shard", None),
        P(),
        P(),
    )
    out_specs = (P("shard", None), P(None, "shard", None), P(None, "shard", None))
    return jax.shard_map(
        per_device, mesh=mesh, in_specs=in_specs, out_specs=out_specs, check_vma=False
    )
```

```python
import functools
import math

import jax
import jax.numpy as jnp
from jax import lax
from jax.experimental import pallas as pl
from jax.experimental.pallas import tpu as pltpu
from jax.sharding import PartitionSpec as P

ITERS = 3


decay_base = 0.9
tiny_term = 1e-06


def from_partner(x, axis, apart):
    return lax.ppermute(x, axis, [(i, i ^ 1 << apart) for i in range(lax.axis_size(axis))])


def as_sent(x):
    return jax.tree.map(lambda a: a.astype(jnp.bfloat16) if a.dtype == jnp.float32 else a, x)


def newton(matrix):
    identity = jnp.eye(matrix.shape[-1], dtype=jnp.float32)
    frobenius = jnp.sqrt(jnp.sum(matrix * matrix) + tiny_term)
    scaling = 2.5 / frobenius
    iterate = scaling**0.25 * identity
    residual_map = scaling * matrix
    for sweep_index in range(ITERS):
        factor = (5.0 * identity - residual_map) * 0.25
        iterate = jnp.matmul(iterate, factor, precision=lax.Precision.HIGHEST)
        square = jnp.matmul(factor, factor, precision=lax.Precision.HIGHEST)
        fourth = jnp.matmul(square, square, precision=lax.Precision.HIGHEST)
        residual_map = jnp.matmul(fourth, residual_map, precision=lax.Precision.HIGHEST)
    return iterate


def gram_pair(blocks):
    left_gram = jnp.einsum("nij,nkj->nik", blocks, blocks, preferred_element_type=jnp.float32)
    right_gram = jnp.einsum("nji,njk->nik", blocks, blocks, preferred_element_type=jnp.float32)
    return jnp.stack([left_gram, right_gram], axis=1)


def stat_swap(values, bit_number):
    return from_partner(values, "shard", bit_number)


def block_swap(values, bit_number):
    return jax.tree.map(
        lambda part, own: part.astype(own.dtype),
        from_partner(as_sent(values), "shard", bit_number),
        values,
    )


def team_block(values, mover, team_size):
    shard_index = lax.axis_index("shard")
    gathered = values
    for bit_number in range(team_size.bit_length() - 1):
        partner = mover(gathered, bit_number)
        upper_side = jnp.right_shift(shard_index, bit_number) % 2 == 1
        below = jnp.concatenate([partner, gathered], axis=1)
        above = jnp.concatenate([gathered, partner], axis=1)
        gathered = jnp.where(upper_side, below, above)
    return gathered


def general(activations, cotangents, statistics, roots, ages, refresh):
    tokens_here = activations.shape[0]
    block_order = activations.shape[1]
    full_width = cotangents.shape[1]
    shards = lax.axis_size("shard")
    copies = lax.axis_size("replica")
    rows_here = statistics.shape[1]
    piece_rows = rows_here // copies
    reordered = (
        cotangents.reshape(tokens_here, shards, copies, piece_rows)
        .transpose(0, 2, 1, 3)
        .reshape(tokens_here, full_width)
    )
    total_piece = lax.psum_scatter(
        lax.dot_general(
            reordered, activations, (((0,), (0,)), ((), ())), preferred_element_type=jnp.float32
        ),
        ("replica", "shard"),
        scatter_dimension=0,
        tiled=True,
    )
    gradient = lax.all_gather(total_piece.astype(jnp.bfloat16), "replica", axis=0, tiled=True)
    shard_index = lax.axis_index("shard")
    if rows_here < block_order:
        team_size = block_order // rows_here
        team_place = shard_index % team_size
        first_block = shard_index // team_size
        row_start = team_place * rows_here
        blocks_here = 1
        old_stats = team_block(statistics, stat_swap, team_size)[:, None]
        full_pair = team_block(jnp.stack([gradient, roots[1]]), block_swap, team_size)
        grad_blocks = full_pair[0][None]
        right_old = full_pair[1][None]

        def own_rows(blocks):
            return lax.dynamic_slice_in_dim(blocks[0], row_start, rows_here, 0)

    else:
        blocks_here = rows_here // block_order
        first_block = shard_index * blocks_here
        old_stats = statistics.reshape(2, blocks_here, block_order, block_order)
        grad_blocks = gradient.reshape(blocks_here, block_order, block_order)
        right_old = roots[1].reshape(blocks_here, block_order, block_order)

        def own_rows(blocks):
            return blocks.reshape(rows_here, blocks.shape[-1])

    count_here = 2 * blocks_here
    gram_pairs = gram_pair(grad_blocks).reshape(count_here, block_order, block_order)
    previous = old_stats.transpose(1, 0, 2, 3).reshape(count_here, block_order, block_order)
    ages_here = lax.dynamic_slice_in_dim(ages, 2 * first_block, count_here, 0)
    fresh_here = lax.dynamic_slice_in_dim(refresh, 2 * first_block, count_here, 0) == 1
    decay_factor = (decay_base ** ages_here.astype(jnp.float32))[:, None, None]
    updated = jnp.where(
        fresh_here[:, None, None],
        decay_factor * previous + (1.0 - decay_factor) * gram_pairs,
        previous,
    )
    refreshed = jax.vmap(newton)(updated).astype(jnp.bfloat16)
    root_pairs = refreshed.reshape(blocks_here, 2, block_order, block_order)
    fresh_pairs = fresh_here.reshape(blocks_here, 2)
    right_full = jnp.where(fresh_pairs[:, 1, None, None], root_pairs[:, 1], right_old)
    left_mask = own_rows(
        jnp.broadcast_to(fresh_pairs[:, 0, None, None], (blocks_here, block_order, 1))
    )
    left_rows = jnp.where(left_mask, own_rows(root_pairs[:, 0]), roots[0])
    new_roots = jnp.stack([left_rows, own_rows(right_full)])
    stat_pairs = updated.reshape(blocks_here, 2, block_order, block_order)
    new_statistics = jnp.stack([own_rows(stat_pairs[:, 0]), own_rows(stat_pairs[:, 1])])
    mixed_blocks = jnp.einsum(
        "nij,njk->nik", grad_blocks, right_full, preferred_element_type=jnp.float32
    ).astype(jnp.bfloat16)
    left_blocks = left_rows.reshape(blocks_here, -1, block_order)
    product = jnp.einsum(
        "nij,njk->nik", left_blocks, mixed_blocks, preferred_element_type=jnp.float32
    )
    update = (product.reshape(rows_here, block_order) * math.sqrt(block_order)).astype(jnp.bfloat16)
    return (update, new_statistics, new_roots)


CORES = 2
LANES = 2
LEVELS = 4
VMEM = 24 << 20
SPLIT = 2
AHEAD = 3
MESH = pl.DeviceIdType.MESH


def exchange_kernel(
    sizes, cot_ref, act_ref, grad_ref, cots, acts, outgoing, incoming, grad,
    local_sem, act_send, act_recv, relay_send, cot_send, cot_recv,
    part_send, part_recv, grad_send, grad_recv,
):
    copies, levels, tokens, rows = sizes
    piece = rows // copies
    part_rows = piece // SPLIT
    team = CORES * LANES
    here = lax.axis_index("replica")
    shard = lax.axis_index("shard")
    level = shard // team
    lane = (shard // CORES) % LANES
    core = shard % CORES
    slots = [(a, b, c) for a in range(copies) for b in range(LANES) for c in range(CORES)]
    steps = [(part, k) for k in range(levels) for part in range(SPLIT)]

    def peer(offset):
        a, b, c = offset
        other = (level * LANES + (lane + b) % LANES) * CORES + (core + c) % CORES
        return ((here + a) % copies, other)

    beside = level + 1 - 2 * (level % 2)
    targets = [(beside + 2) % levels, (level + 2) % levels, beside, level]
    receivers = [beside, (level + 2) % levels, beside]

    def level_peer(other):
        return (here, other * team + lane * CORES + core)

    def columns(device, part, k):
        target = targets[k] * team + device[1] % team
        start = target * rows + device[0] * piece + part * part_rows
        return pl.ds(pl.multiple_of(start, part_rows), part_rows)

    def token_rows(index):
        return pl.ds(index * tokens, tokens)

    barrier = pltpu.get_barrier_semaphore()
    for offset in slots[1:]:
        pl.semaphore_signal(barrier, inc=1, device_id=peer(offset), device_id_type=MESH)
    for other in receivers[:2]:
        pl.semaphore_signal(barrier, inc=1, device_id=level_peer(other), device_id_type=MESH)
    own_act = pltpu.make_async_copy(act_ref, acts.at[token_rows(0)], local_sem.at[0])
    own_act.start()
    own_cots = []
    for turn, (part, k) in enumerate(steps):
        own = pltpu.make_async_copy(
            cot_ref.at[:, columns((here, shard), part, k)],
            cots.at[turn, token_rows(0)],
            local_sem.at[1 + turn],
        )
        own.start()
        own_cots.append(own)
    pl.semaphore_wait(barrier, len(slots) - 1 + 2)

    sends = []

    def send_act(offset, direct, via):
        index = slots.index(offset)
        first = slots.index(tuple(o - v for o, v in zip(offset, via)))
        copy = pltpu.make_async_remote_copy(
            src_ref=act_ref if direct else acts.at[token_rows(first)],
            dst_ref=acts.at[token_rows(index)],
            send_sem=act_send.at[index],
            recv_sem=act_recv.at[index],
            device_id=peer(via),
            device_id_type=MESH,
        )
        copy.start()
        sends.append(copy)
        return copy

    cot_in = {}

    def send_cots(turns):
        for turn in turns:
            for index in range(1, len(slots)):
                device = peer(slots[index])
                copy = pltpu.make_async_remote_copy(
                    src_ref=cot_ref.at[:, columns(device, *steps[turn])],
                    dst_ref=cots.at[turn, token_rows(index)],
                    send_sem=cot_send.at[turn, index],
                    recv_sem=cot_recv.at[turn, index],
                    device_id=device,
                    device_id_type=MESH,
                )
                copy.start()
                sends.append(copy)
                cot_in[turn, index] = copy

    act_in = {}
    for offset in slots[1:]:
        if not offset[2] or offset[:2] == (0, 0):
            act_in[offset] = send_act(offset, True, offset)
    send_cots(range(AHEAD))
    for a, b, c in slots[1:]:
        if c and (a or b):
            if c == 1:
                act_in[a, b, 0].wait_recv()
            act_in[a, b, c] = send_act((a, b, c), False, (0, 0, c))
    own_act.wait()
    for offset in slots:
        if offset[2]:
            act_in[offset].wait_recv()

    parts, finals = {}, []
    for turn, (part, k) in enumerate(steps):
        own_cots[turn].wait()
        for index in range(1, len(slots)):
            cot_in[turn, index].wait_recv()
        term = lax.dot_general(
            cots[turn], acts[...], (((0,), (0,)), ((), ())), preferred_element_type=jnp.float32
        )
        if k == 1:
            parts[part, 0].wait_recv()
            term += incoming[part].astype(jnp.float32)
        if k < levels - 1:
            outgoing[turn] = term.astype(jnp.bfloat16)
            copy = pltpu.make_async_remote_copy(
                src_ref=outgoing.at[turn],
                dst_ref=incoming.at[turn],
                send_sem=part_send.at[turn],
                recv_sem=part_recv.at[turn],
                device_id=level_peer(receivers[k]),
                device_id_type=MESH,
            )
            copy.start()
            sends.append(copy)
            parts[part, k] = copy
            send_cots(range(turn + AHEAD, min(turn + AHEAD + 1, len(steps))))
            continue
        for other in range(1, k):
            parts[part, other].wait_recv()
            term += incoming[other * SPLIT + part].astype(jnp.float32)
        start = here * piece + part * part_rows
        mine = pl.ds(pl.multiple_of(start, part_rows), part_rows)
        grad[mine] = term.astype(jnp.bfloat16)
        for step in range(1, copies):
            copy = pltpu.make_async_remote_copy(
                src_ref=grad.at[mine],
                dst_ref=grad.at[mine],
                send_sem=grad_send.at[part, step],
                recv_sem=grad_recv.at[part, step],
                device_id=((here + step) % copies, shard),
                device_id_type=MESH,
            )
            copy.start()
            finals.append(copy)
    for copy in sends:
        copy.wait_send()
    for copy in finals:
        copy.wait()
    grad_ref[...] = grad[...]


def pinned(x):
    return pltpu.with_memory_space_constraint(x, pltpu.HBM)


def exchange(cotangents, activations, copies, levels, rows):
    tokens, block = activations.shape
    team = CORES * LANES
    many = copies * team
    turns = SPLIT * levels
    part_rows = rows // copies // SPLIT
    dma = pltpu.SemaphoreType.DMA
    return pl.pallas_call(
        functools.partial(exchange_kernel, (copies, levels, tokens, rows)),
        out_shape=jax.ShapeDtypeStruct((rows, block), jnp.bfloat16),
        in_specs=[pl.BlockSpec(memory_space=pltpu.HBM)] * 2,
        out_specs=pl.BlockSpec(memory_space=pltpu.VMEM),
        scratch_shapes=[
            pltpu.VMEM((turns, many * tokens, part_rows), jnp.bfloat16),
            pltpu.VMEM((many * tokens, block), jnp.bfloat16),
            pltpu.VMEM((turns, part_rows, block), jnp.bfloat16),
            pltpu.VMEM((turns, part_rows, block), jnp.bfloat16),
            pltpu.VMEM((rows, block), jnp.bfloat16),
            dma((1 + turns,)),
            dma((many,)),
            dma((many,)),
            dma((many,)),
            dma((turns, many)),
            dma((turns, many)),
            dma((turns,)),
            dma((turns,)),
            dma((SPLIT, copies)),
            dma((SPLIT, copies)),
        ],
        compiler_params=pltpu.CompilerParams(collective_id=0, has_side_effects=True, vmem_limit_bytes=VMEM),
        name="exchange",
    )(pinned(cotangents), pinned(activations))


def product(left, right, contract=((1,), (0,))):
    return lax.dot_general(left, right, (contract, ((), ())), preferred_element_type=jnp.float32)


def small(x):
    return x.astype(jnp.bfloat16)


def root_step(n):
    half = small(n)
    q = product(half, half) - 2.5 * n
    half_q = small(q)
    r = product(half_q, half_q) + 3.125 * q
    return product(small(r), half) + 1.25**4 * n


def refresh_kernel(grad_ref, stats_ref, roots_ref, ages_ref, fresh_ref,
                   update_out, new_stats_out, new_roots_out,
                   update_ref, new_stats_ref, new_roots_ref, old_roots_ref, sem):
    old_roots = pltpu.make_async_copy(roots_ref, old_roots_ref, sem.at[5])
    old_roots.start()
    pending = []

    def put(source, target):
        copy = pltpu.make_async_copy(source, target, sem.at[len(pending)])
        copy.start()
        pending.append(copy)

    first = 2 * lax.axis_index("shard")
    block = grad_ref.shape[0]
    grad = grad_ref[...]
    grams = [lambda: product(grad, grad, ((1,), (1,))), lambda: product(grad, grad, ((0,), (0,)))]
    maps, scales, fresh = [], [], []
    for side in range(2):
        is_fresh = fresh_ref[first + side] == 1
        age = jnp.full((1, 1), ages_ref[first + side].astype(jnp.float32), jnp.float32)
        decay = jnp.exp(age * math.log(decay_base))
        gram = grams[side]()
        old = stats_ref[side]
        new = jnp.where(is_fresh, decay * old + (1.0 - decay) * gram, old)
        new_stats_ref[side] = new
        put(new_stats_ref.at[side], new_stats_out.at[side])
        total = jnp.sum(jnp.sum(new * new, axis=0, keepdims=True), axis=1, keepdims=True)
        scaling = 2.5 / jnp.sqrt(total + tiny_term)
        maps.append((0.25 * scaling) * new)
        scales.append(jnp.sqrt(jnp.sqrt(scaling)))
        fresh.append(is_fresh)
    n1 = maps
    n2 = [root_step(n) for n in n1]
    x2 = [product(small(a), small(b)) - 1.25 * (a + b) for a, b in zip(n1, n2)]
    n3 = [root_step(n) for n in n2]
    row = lax.broadcasted_iota(jnp.int32, (block, block), 0)
    column = lax.broadcasted_iota(jnp.int32, (block, block), 1)
    diagonal = jnp.where(row == column, 1.25**3, 0.0)
    roots = []
    old_roots.wait()
    for side in range(2):
        last = diagonal + 1.25 * x2[side] - 1.5625 * n3[side]
        last = last - product(small(x2[side]), small(n3[side]))
        root = small(scales[side] * last)
        root = jnp.where(fresh[side], root, old_roots_ref[side])
        new_roots_ref[side] = root
        put(new_roots_ref.at[side], new_roots_out.at[side])
        roots.append(root)
    mixed = small(product(grad, roots[1]))
    update_ref[...] = small(product(roots[0], mixed) * math.sqrt(block))
    put(update_ref, update_out)
    for copy in pending:
        copy.wait()


def refresh_roots(gradient, statistics, roots, ages, refresh):
    vmem = pl.BlockSpec(memory_space=pltpu.VMEM)
    smem = pl.BlockSpec(memory_space=pltpu.SMEM)
    hbm = pl.BlockSpec(memory_space=pltpu.HBM)
    return pl.pallas_call(
        refresh_kernel,
        out_shape=(
            jax.ShapeDtypeStruct(gradient.shape, jnp.bfloat16),
            jax.ShapeDtypeStruct(statistics.shape, jnp.float32),
            jax.ShapeDtypeStruct(roots.shape, jnp.bfloat16),
        ),
        in_specs=[vmem, vmem, hbm, smem, smem],
        out_specs=(hbm,) * 3,
        scratch_shapes=[
            pltpu.VMEM(gradient.shape, jnp.bfloat16),
            pltpu.VMEM(statistics.shape, jnp.float32),
            pltpu.VMEM(roots.shape, jnp.bfloat16),
            pltpu.VMEM(roots.shape, jnp.bfloat16),
            pltpu.SemaphoreType.DMA((6,)),
        ],
        compiler_params=pltpu.CompilerParams(vmem_limit_bytes=VMEM),
        name="refresh_roots",
    )(gradient, statistics, pinned(roots), ages, refresh)


def per_device(activations, cotangents, statistics, roots, ages, refresh):
    shards = lax.axis_size("shard")
    copies = lax.axis_size("replica")
    rows = statistics.shape[1]
    block = activations.shape[1]
    team = CORES * LANES
    if rows != block or shards != LEVELS * team or rows % copies or (rows // copies) % (128 * SPLIT):
        return general(activations, cotangents, statistics, roots, ages, refresh)
    gradient = exchange(cotangents, activations, copies, shards // team, rows)
    return refresh_roots(gradient, statistics, roots, ages, refresh)


def solution(mesh):
    in_specs = (
        P(("replica", "shard"), None),
        P(("replica", "shard"), None),
        P(None, "shard", None),
        P(None, "shard", None),
        P(),
        P(),
    )
    out_specs = (P("shard", None), P(None, "shard", None), P(None, "shard", None))
    return jax.shard_map(
        per_device, mesh=mesh, in_specs=in_specs, out_specs=out_specs, check_vma=False
    )
```

```python
import functools
import math

import jax
import jax.numpy as jnp
from jax import lax
from jax.experimental import pallas as pl
from jax.experimental.pallas import tpu as pltpu
from jax.sharding import PartitionSpec as P

ITERS = 3


decay_base = 0.9
tiny_term = 1e-06


def from_partner(x, axis, apart):
    return lax.ppermute(x, axis, [(i, i ^ 1 << apart) for i in range(lax.axis_size(axis))])


def as_sent(x):
    return jax.tree.map(lambda a: a.astype(jnp.bfloat16) if a.dtype == jnp.float32 else a, x)


def newton(matrix):
    identity = jnp.eye(matrix.shape[-1], dtype=jnp.float32)
    frobenius = jnp.sqrt(jnp.sum(matrix * matrix) + tiny_term)
    scaling = 2.5 / frobenius
    iterate = scaling**0.25 * identity
    residual_map = scaling * matrix
    for sweep_index in range(ITERS):
        factor = (5.0 * identity - residual_map) * 0.25
        iterate = jnp.matmul(iterate, factor, precision=lax.Precision.HIGHEST)
        square = jnp.matmul(factor, factor, precision=lax.Precision.HIGHEST)
        fourth = jnp.matmul(square, square, precision=lax.Precision.HIGHEST)
        residual_map = jnp.matmul(fourth, residual_map, precision=lax.Precision.HIGHEST)
    return iterate


def gram_pair(blocks):
    left_gram = jnp.einsum("nij,nkj->nik", blocks, blocks, preferred_element_type=jnp.float32)
    right_gram = jnp.einsum("nji,njk->nik", blocks, blocks, preferred_element_type=jnp.float32)
    return jnp.stack([left_gram, right_gram], axis=1)


def stat_swap(values, bit_number):
    return from_partner(values, "shard", bit_number)


def block_swap(values, bit_number):
    return jax.tree.map(
        lambda part, own: part.astype(own.dtype),
        from_partner(as_sent(values), "shard", bit_number),
        values,
    )


def team_block(values, mover, team_size):
    shard_index = lax.axis_index("shard")
    gathered = values
    for bit_number in range(team_size.bit_length() - 1):
        partner = mover(gathered, bit_number)
        upper_side = jnp.right_shift(shard_index, bit_number) % 2 == 1
        below = jnp.concatenate([partner, gathered], axis=1)
        above = jnp.concatenate([gathered, partner], axis=1)
        gathered = jnp.where(upper_side, below, above)
    return gathered


def general(activations, cotangents, statistics, roots, ages, refresh):
    tokens_here = activations.shape[0]
    block_order = activations.shape[1]
    full_width = cotangents.shape[1]
    shards = lax.axis_size("shard")
    copies = lax.axis_size("replica")
    rows_here = statistics.shape[1]
    piece_rows = rows_here // copies
    reordered = (
        cotangents.reshape(tokens_here, shards, copies, piece_rows)
        .transpose(0, 2, 1, 3)
        .reshape(tokens_here, full_width)
    )
    total_piece = lax.psum_scatter(
        lax.dot_general(
            reordered, activations, (((0,), (0,)), ((), ())), preferred_element_type=jnp.float32
        ),
        ("replica", "shard"),
        scatter_dimension=0,
        tiled=True,
    )
    gradient = lax.all_gather(total_piece.astype(jnp.bfloat16), "replica", axis=0, tiled=True)
    shard_index = lax.axis_index("shard")
    if rows_here < block_order:
        team_size = block_order // rows_here
        team_place = shard_index % team_size
        first_block = shard_index // team_size
        row_start = team_place * rows_here
        blocks_here = 1
        old_stats = team_block(statistics, stat_swap, team_size)[:, None]
        full_pair = team_block(jnp.stack([gradient, roots[1]]), block_swap, team_size)
        grad_blocks = full_pair[0][None]
        right_old = full_pair[1][None]

        def own_rows(blocks):
            return lax.dynamic_slice_in_dim(blocks[0], row_start, rows_here, 0)

    else:
        blocks_here = rows_here // block_order
        first_block = shard_index * blocks_here
        old_stats = statistics.reshape(2, blocks_here, block_order, block_order)
        grad_blocks = gradient.reshape(blocks_here, block_order, block_order)
        right_old = roots[1].reshape(blocks_here, block_order, block_order)

        def own_rows(blocks):
            return blocks.reshape(rows_here, blocks.shape[-1])

    count_here = 2 * blocks_here
    gram_pairs = gram_pair(grad_blocks).reshape(count_here, block_order, block_order)
    previous = old_stats.transpose(1, 0, 2, 3).reshape(count_here, block_order, block_order)
    ages_here = lax.dynamic_slice_in_dim(ages, 2 * first_block, count_here, 0)
    fresh_here = lax.dynamic_slice_in_dim(refresh, 2 * first_block, count_here, 0) == 1
    decay_factor = (decay_base ** ages_here.astype(jnp.float32))[:, None, None]
    updated = jnp.where(
        fresh_here[:, None, None],
        decay_factor * previous + (1.0 - decay_factor) * gram_pairs,
        previous,
    )
    refreshed = jax.vmap(newton)(updated).astype(jnp.bfloat16)
    root_pairs = refreshed.reshape(blocks_here, 2, block_order, block_order)
    fresh_pairs = fresh_here.reshape(blocks_here, 2)
    right_full = jnp.where(fresh_pairs[:, 1, None, None], root_pairs[:, 1], right_old)
    left_mask = own_rows(
        jnp.broadcast_to(fresh_pairs[:, 0, None, None], (blocks_here, block_order, 1))
    )
    left_rows = jnp.where(left_mask, own_rows(root_pairs[:, 0]), roots[0])
    new_roots = jnp.stack([left_rows, own_rows(right_full)])
    stat_pairs = updated.reshape(blocks_here, 2, block_order, block_order)
    new_statistics = jnp.stack([own_rows(stat_pairs[:, 0]), own_rows(stat_pairs[:, 1])])
    mixed_blocks = jnp.einsum(
        "nij,njk->nik", grad_blocks, right_full, preferred_element_type=jnp.float32
    ).astype(jnp.bfloat16)
    left_blocks = left_rows.reshape(blocks_here, -1, block_order)
    product = jnp.einsum(
        "nij,njk->nik", left_blocks, mixed_blocks, preferred_element_type=jnp.float32
    )
    update = (product.reshape(rows_here, block_order) * math.sqrt(block_order)).astype(jnp.bfloat16)
    return (update, new_statistics, new_roots)


CORES = 2
LANES = 2
LEVELS = 4
VMEM = 24 << 20
SPLIT = 2
AHEAD = 3
MESH = pl.DeviceIdType.MESH


def exchange_kernel(
    sizes, cot_ref, act_ref, grad_ref, cots, acts, outgoing, incoming, grad,
    local_sem, act_send, act_recv, relay_send, cot_send, cot_recv,
    part_send, part_recv, grad_send, grad_recv,
):
    copies, levels, tokens, rows = sizes
    piece = rows // copies
    part_rows = piece // SPLIT
    team = CORES * LANES
    here = lax.axis_index("replica")
    shard = lax.axis_index("shard")
    level = shard // team
    lane = (shard // CORES) % LANES
    core = shard % CORES
    slots = [(a, b, c) for a in range(copies) for b in range(LANES) for c in range(CORES)]
    steps = [(part, 0) for part in range(SPLIT)]
    steps += [(part, k) for part in range(SPLIT) for k in range(1, levels - 1)]
    steps += [(part, levels - 1) for part in range(SPLIT)]

    def peer(offset):
        a, b, c = offset
        other = (level * LANES + (lane + b) % LANES) * CORES + (core + c) % CORES
        return ((here + a) % copies, other)

    beside = level + 1 - 2 * (level % 2)
    targets = [(beside + 2) % levels, (level + 2) % levels, beside, level]
    receivers = [beside, (level + 2) % levels, beside]

    def level_peer(other):
        return (here, other * team + lane * CORES + core)

    def columns(device, part, k):
        target = targets[k] * team + device[1] % team
        start = target * rows + device[0] * piece + part * part_rows
        return pl.ds(pl.multiple_of(start, part_rows), part_rows)

    def token_rows(index):
        return pl.ds(index * tokens, tokens)

    barrier = pltpu.get_barrier_semaphore()
    for offset in slots[1:]:
        pl.semaphore_signal(barrier, inc=1, device_id=peer(offset), device_id_type=MESH)
    for other in receivers[:2]:
        pl.semaphore_signal(barrier, inc=1, device_id=level_peer(other), device_id_type=MESH)
    own_act = pltpu.make_async_copy(act_ref, acts.at[token_rows(0)], local_sem.at[0])
    own_act.start()
    own_cots = []
    for turn, (part, k) in enumerate(steps):
        own = pltpu.make_async_copy(
            cot_ref.at[:, columns((here, shard), part, k)],
            cots.at[turn, token_rows(0)],
            local_sem.at[1 + turn],
        )
        own.start()
        own_cots.append(own)
    pl.semaphore_wait(barrier, len(slots) - 1 + 2)

    sends = []

    def send_act(offset, direct, via):
        index = slots.index(offset)
        first = slots.index(tuple(o - v for o, v in zip(offset, via)))
        copy = pltpu.make_async_remote_copy(
            src_ref=act_ref if direct else acts.at[token_rows(first)],
            dst_ref=acts.at[token_rows(index)],
            send_sem=act_send.at[index],
            recv_sem=act_recv.at[index],
            device_id=peer(via),
            device_id_type=MESH,
        )
        copy.start()
        sends.append(copy)
        return copy

    cot_in = {}

    def send_cots(turns):
        for turn in turns:
            for index in range(1, len(slots)):
                device = peer(slots[index])
                copy = pltpu.make_async_remote_copy(
                    src_ref=cot_ref.at[:, columns(device, *steps[turn])],
                    dst_ref=cots.at[turn, token_rows(index)],
                    send_sem=cot_send.at[turn, index],
                    recv_sem=cot_recv.at[turn, index],
                    device_id=device,
                    device_id_type=MESH,
                )
                copy.start()
                sends.append(copy)
                cot_in[turn, index] = copy

    act_in = {}
    for offset in slots[1:]:
        if not offset[2] or offset[:2] == (0, 0):
            act_in[offset] = send_act(offset, True, offset)
    send_cots(range(AHEAD))
    for a, b, c in slots[1:]:
        if c and (a or b):
            if c == 1:
                act_in[a, b, 0].wait_recv()
            act_in[a, b, c] = send_act((a, b, c), False, (0, 0, c))
    own_act.wait()
    for offset in slots:
        if offset[2]:
            act_in[offset].wait_recv()

    parts, finals = {}, []
    for turn, (part, k) in enumerate(steps):
        own_cots[turn].wait()
        for index in range(1, len(slots)):
            cot_in[turn, index].wait_recv()
        term = lax.dot_general(
            cots[turn], acts[...], (((0,), (0,)), ((), ())), preferred_element_type=jnp.float32
        )
        if k == 1:
            parts[part, 0].wait_recv()
            term += incoming[steps.index((part, 0))].astype(jnp.float32)
        if k < levels - 1:
            outgoing[turn] = term.astype(jnp.bfloat16)
            copy = pltpu.make_async_remote_copy(
                src_ref=outgoing.at[turn],
                dst_ref=incoming.at[turn],
                send_sem=part_send.at[turn],
                recv_sem=part_recv.at[turn],
                device_id=level_peer(receivers[k]),
                device_id_type=MESH,
            )
            copy.start()
            sends.append(copy)
            parts[part, k] = copy
            send_cots(range(turn + AHEAD, min(turn + AHEAD + 1, len(steps))))
            continue
        for other in range(1, k):
            parts[part, other].wait_recv()
            term += incoming[steps.index((part, other))].astype(jnp.float32)
        start = here * piece + part * part_rows
        mine = pl.ds(pl.multiple_of(start, part_rows), part_rows)
        grad[mine] = term.astype(jnp.bfloat16)
        for step in range(1, copies):
            copy = pltpu.make_async_remote_copy(
                src_ref=grad.at[mine],
                dst_ref=grad.at[mine],
                send_sem=grad_send.at[part, step],
                recv_sem=grad_recv.at[part, step],
                device_id=((here + step) % copies, shard),
                device_id_type=MESH,
            )
            copy.start()
            finals.append(copy)
    for copy in sends:
        copy.wait_send()
    for copy in finals:
        copy.wait()
    grad_ref[...] = grad[...]


def pinned(x):
    return pltpu.with_memory_space_constraint(x, pltpu.HBM)


def exchange(cotangents, activations, copies, levels, rows):
    tokens, block = activations.shape
    team = CORES * LANES
    many = copies * team
    turns = SPLIT * levels
    part_rows = rows // copies // SPLIT
    dma = pltpu.SemaphoreType.DMA
    return pl.pallas_call(
        functools.partial(exchange_kernel, (copies, levels, tokens, rows)),
        out_shape=jax.ShapeDtypeStruct((rows, block), jnp.bfloat16),
        in_specs=[pl.BlockSpec(memory_space=pltpu.HBM)] * 2,
        out_specs=pl.BlockSpec(memory_space=pltpu.VMEM),
        scratch_shapes=[
            pltpu.VMEM((turns, many * tokens, part_rows), jnp.bfloat16),
            pltpu.VMEM((many * tokens, block), jnp.bfloat16),
            pltpu.VMEM((turns, part_rows, block), jnp.bfloat16),
            pltpu.VMEM((turns, part_rows, block), jnp.bfloat16),
            pltpu.VMEM((rows, block), jnp.bfloat16),
            dma((1 + turns,)),
            dma((many,)),
            dma((many,)),
            dma((many,)),
            dma((turns, many)),
            dma((turns, many)),
            dma((turns,)),
            dma((turns,)),
            dma((SPLIT, copies)),
            dma((SPLIT, copies)),
        ],
        compiler_params=pltpu.CompilerParams(collective_id=0, has_side_effects=True, vmem_limit_bytes=VMEM),
        name="exchange",
    )(pinned(cotangents), pinned(activations))


def product(left, right, contract=((1,), (0,))):
    return lax.dot_general(left, right, (contract, ((), ())), preferred_element_type=jnp.float32)


def small(x):
    return x.astype(jnp.bfloat16)


def root_step(n):
    half = small(n)
    q = product(half, half) - 2.5 * n
    half_q = small(q)
    r = product(half_q, half_q) + 3.125 * q
    return product(small(r), half) + 1.25**4 * n


def refresh_kernel(grad_ref, stats_ref, roots_ref, ages_ref, fresh_ref,
                   update_out, new_stats_out, new_roots_out,
                   update_ref, new_stats_ref, new_roots_ref, old_roots_ref, sem):
    old_roots = pltpu.make_async_copy(roots_ref, old_roots_ref, sem.at[5])
    old_roots.start()
    pending = []

    def put(source, target):
        copy = pltpu.make_async_copy(source, target, sem.at[len(pending)])
        copy.start()
        pending.append(copy)

    first = 2 * lax.axis_index("shard")
    block = grad_ref.shape[0]
    grad = grad_ref[...]
    grams = [lambda: product(grad, grad, ((1,), (1,))), lambda: product(grad, grad, ((0,), (0,)))]
    maps, scales, fresh = [], [], []
    for side in range(2):
        is_fresh = fresh_ref[first + side] == 1
        age = jnp.full((1, 1), ages_ref[first + side].astype(jnp.float32), jnp.float32)
        decay = jnp.exp(age * math.log(decay_base))
        gram = grams[side]()
        old = stats_ref[side]
        new = jnp.where(is_fresh, decay * old + (1.0 - decay) * gram, old)
        new_stats_ref[side] = new
        put(new_stats_ref.at[side], new_stats_out.at[side])
        total = jnp.sum(jnp.sum(new * new, axis=0, keepdims=True), axis=1, keepdims=True)
        scaling = 2.5 / jnp.sqrt(total + tiny_term)
        maps.append((0.25 * scaling) * new)
        scales.append(jnp.sqrt(jnp.sqrt(scaling)))
        fresh.append(is_fresh)
    n1 = maps
    n2 = [root_step(n) for n in n1]
    x2 = [product(small(a), small(b)) - 1.25 * (a + b) for a, b in zip(n1, n2)]
    n3 = [root_step(n) for n in n2]
    row = lax.broadcasted_iota(jnp.int32, (block, block), 0)
    column = lax.broadcasted_iota(jnp.int32, (block, block), 1)
    diagonal = jnp.where(row == column, 1.25**3, 0.0)
    roots = []
    old_roots.wait()
    for side in range(2):
        last = diagonal + 1.25 * x2[side] - 1.5625 * n3[side]
        last = last - product(small(x2[side]), small(n3[side]))
        root = small(scales[side] * last)
        root = jnp.where(fresh[side], root, old_roots_ref[side])
        new_roots_ref[side] = root
        put(new_roots_ref.at[side], new_roots_out.at[side])
        roots.append(root)
    mixed = small(product(grad, roots[1]))
    update_ref[...] = small(product(roots[0], mixed) * math.sqrt(block))
    put(update_ref, update_out)
    for copy in pending:
        copy.wait()


def refresh_roots(gradient, statistics, roots, ages, refresh):
    vmem = pl.BlockSpec(memory_space=pltpu.VMEM)
    smem = pl.BlockSpec(memory_space=pltpu.SMEM)
    hbm = pl.BlockSpec(memory_space=pltpu.HBM)
    return pl.pallas_call(
        refresh_kernel,
        out_shape=(
            jax.ShapeDtypeStruct(gradient.shape, jnp.bfloat16),
            jax.ShapeDtypeStruct(statistics.shape, jnp.float32),
            jax.ShapeDtypeStruct(roots.shape, jnp.bfloat16),
        ),
        in_specs=[vmem, vmem, hbm, smem, smem],
        out_specs=(hbm,) * 3,
        scratch_shapes=[
            pltpu.VMEM(gradient.shape, jnp.bfloat16),
            pltpu.VMEM(statistics.shape, jnp.float32),
            pltpu.VMEM(roots.shape, jnp.bfloat16),
            pltpu.VMEM(roots.shape, jnp.bfloat16),
            pltpu.SemaphoreType.DMA((6,)),
        ],
        compiler_params=pltpu.CompilerParams(vmem_limit_bytes=VMEM),
        name="refresh_roots",
    )(gradient, statistics, pinned(roots), ages, refresh)


def per_device(activations, cotangents, statistics, roots, ages, refresh):
    shards = lax.axis_size("shard")
    copies = lax.axis_size("replica")
    rows = statistics.shape[1]
    block = activations.shape[1]
    team = CORES * LANES
    if rows != block or shards != LEVELS * team or rows % copies or (rows // copies) % (128 * SPLIT):
        return general(activations, cotangents, statistics, roots, ages, refresh)
    gradient = exchange(cotangents, activations, copies, shards // team, rows)
    return refresh_roots(gradient, statistics, roots, ages, refresh)


def solution(mesh):
    in_specs = (
        P(("replica", "shard"), None),
        P(("replica", "shard"), None),
        P(None, "shard", None),
        P(None, "shard", None),
        P(),
        P(),
    )
    out_specs = (P("shard", None), P(None, "shard", None), P(None, "shard", None))
    return jax.shard_map(
        per_device, mesh=mesh, in_specs=in_specs, out_specs=out_specs, check_vma=False
    )
```
